32 devices in a mesh: dp: 16 (over z, x, core), fsdp: 2 (over y).
Axes of the slice: x: 2, y: 2, z: 4, core: 2. Of those that a mesh axis runs over, the one named last changes fastest.
Arguments:
- tokens: bfloat16 [4096, 1024], P(('dp', 'fsdp')), may hold values from -6 to 6
- lengths: int32 [32], P(('dp', 'fsdp')), may hold values from 16 to 128, as said below
- cotangent: bfloat16 [4096, 1024], P(('dp', 'fsdp')), may hold values from -6 to 6
- norm_gain: bfloat16 [2, 1024], P(None, 'fsdp'), may hold values from 0.5 to 1.5
- in_proj: bfloat16 [2, 1024, 2, 2048], P(None, None, None, 'fsdp'), may hold values from -0.1875 to 0.1875
- conv_kernel: bfloat16 [2, 4, 2048], P(None, None, 'fsdp'), may hold values from -3 to 3
- conv_bias: bfloat16 [2, 2048], P(None, 'fsdp'), may hold values from -0.5 to 0.5
- x_proj: bfloat16 [2, 96, 2048], P(None, None, 'fsdp'), may hold values from -0.125 to 0.125
- step_proj: bfloat16 [2, 64, 2048], P(None, None, 'fsdp'), may hold values from -0.75 to 0.75
- step_bias: bfloat16 [2, 2048], P(None, 'fsdp'), may hold values from -5 to -2
- decay_log: bfloat16 [2, 16, 2048], P(None, None, 'fsdp'), may hold values from 0 to 2.796875
- skip_gain: bfloat16 [2, 2048], P(None, 'fsdp'), may hold values from 0.5 to 1.5
- out_proj: bfloat16 [2, 2048, 1024], P(None, 'fsdp'), may hold values from -0.375 to 0.375
Outputs:
- mixed: bfloat16 [4096, 1024], P(('dp', 'fsdp'))
- tokens_grad: float32 [4096, 1024], P(('dp', 'fsdp'))
- norm_gain_grad: float32 [2, 1024], P(None, 'fsdp')
- in_proj_grad: float32 [2, 1024, 2, 2048], P(None, None, None, 'fsdp')
- conv_kernel_grad: float32 [2, 4, 2048], P(None, None, 'fsdp')
- conv_bias_grad: float32 [2, 2048], P(None, 'fsdp')
- x_proj_grad: float32 [2, 96, 2048], P(None, None, 'fsdp')
- step_proj_grad: float32 [2, 64, 2048], P(None, None, 'fsdp')
- step_bias_grad: float32 [2, 2048], P(None, 'fsdp')
- decay_log_grad: float32 [2, 16, 2048], P(None, None, 'fsdp')
- skip_gain_grad: float32 [2, 2048], P(None, 'fsdp')
- out_proj_grad: float32 [2, 2048, 1024], P(None, 'fsdp')
The draws below stay inside these ranges and needn't reach their ends.
Inputs may be any that keep to these rules, and one draw needn't show every extreme that they name: `lengths`: count of real tokens in each cluster; the slots after it are padding, and at least one cluster is full.
All inputs are finite; a program needn't handle non-finite values.
Results may differ from the reference program's by a relative error of at most 0.023.
Values may be sent and summed in bfloat16 or wider, within the bound.
No kernel may reach another device: no remote copies, remote signals or barrier semaphores. Data moves between devices by JAX's collectives and lax.ppermute only.
A program may use at most 192 MiB of HBM per device.

```python
from functools import partial
import jax
import jax.numpy as jnp
from jax import lax

D = 1024
E = 2048
N = 16
K = 4
R = 64
LAYERS = 2
SPAN = 16
SLOTS = 128
CLUSTERS = 32
TOKENS = 4096


def draw_lengths(key, part):
    filled = jax.random.randint(jax.random.fold_in(key, 11), (CLUSTERS,), SLOTS // 8, SLOTS + 1)
    full_at = jax.random.randint(jax.random.fold_in(key, 12), (), 0, CLUSTERS)
    return jnp.where(jnp.arange(CLUSTERS, dtype=jnp.int32) == full_at, SLOTS, filled).astype(jnp.int32)


def block_scale(stream_key, extent, shards, least, largest):
    level = 1.0
    for dim, shards_of in shards:
        heights = jax.random.uniform(jax.random.fold_in(jax.random.fold_in(stream_key, 6), dim), (shards_of,), jnp.float32, least / len(shards), largest / len(shards))
        level = level * jnp.repeat(jnp.exp(heights), extent[dim] // shards_of).reshape((-1,) + (1,) * (len(extent) - 1 - dim))
    return level


def bell_draw(stream_key, shape, width, most, pieces=(), kind=jnp.bfloat16):
    gain = block_scale(stream_key, shape, pieces, -0.22, 0.18) if pieces else 1.0
    values = jax.random.normal(stream_key, shape, jnp.float32) * width * gain
    return jnp.minimum(jnp.maximum(values, -most), most).astype(kind)


def setup_inputs(seed: int = 0) -> dict:
    key_list = jax.random.split(jax.random.key(seed), 14)
    return {
        "tokens": bell_draw(key_list[0], (TOKENS, D), 1.0, 6.0, ((0, 32),)),
        "lengths": draw_lengths(jax.random.fold_in(key_list[13], 71), 0),
        "cotangent": bell_draw(key_list[2], (TOKENS, D), 1.0, 6.0, ((0, 32),)),
        "norm_gain": jnp.clip(1.0 + 0.1 * jax.random.normal(key_list[3], (LAYERS, D), jnp.float32), 0.5, 1.5).astype(jnp.bfloat16),
        "in_proj": bell_draw(key_list[4], (LAYERS, D, 2, E), D ** -0.5, 0.1875, ((3, 2),)),
        "conv_kernel": bell_draw(key_list[5], (LAYERS, K, E), K ** -0.5, 3.0, ((2, 2),)),
        "conv_bias": jnp.clip(jax.random.uniform(key_list[6], (LAYERS, E), jnp.float32, -0.5, 0.5) * block_scale(key_list[6], (LAYERS, E), ((1, 2),), -0.4, 0.0), -0.5, 0.5).astype(jnp.bfloat16),
        "x_proj": bell_draw(key_list[7], (LAYERS, R + 2 * N, E), E ** -0.5, 0.125, ((2, 2),)),
        "step_proj": bell_draw(key_list[8], (LAYERS, R, E), R ** -0.5, 0.75, ((2, 2),)),
        "step_bias": jnp.clip(-5.0 + 3.0 * jax.random.uniform(key_list[9], (LAYERS, E), jnp.float32) ** block_scale(key_list[9], (LAYERS, E), ((1, 2),), -0.2, 0.2), -5.0, -2.0).astype(jnp.bfloat16),
        "decay_log": jnp.clip(2.796875 * jax.random.uniform(key_list[10], (LAYERS, N, E), jnp.float32) ** block_scale(key_list[10], (LAYERS, N, E), ((2, 2),), -0.2, 0.2), 0.0, 2.796875).astype(jnp.bfloat16),
        "skip_gain": jnp.clip(0.5 + 1.0 * jax.random.uniform(key_list[11], (LAYERS, E), jnp.float32) ** block_scale(key_list[11], (LAYERS, E), ((1, 2),), -0.2, 0.2), 0.5, 1.5).astype(jnp.bfloat16),
        "out_proj": bell_draw(key_list[12], (LAYERS, E, D), (E // 8) ** -0.5, 0.375, ((1, 2),)),
    }


epsilon = 1e-05

@jax.custom_vjp
def low(v):
    return lax.optimization_barrier(v.astype(jnp.bfloat16)).astype(jnp.float32)

@jax.custom_vjp
def low_back(v):
    return v

def low_keep(v):
    return (low(v), None)

def low_pass(kept, grad):
    return (grad,)

def back_keep(v):
    return (v, None)

def back_low(kept, grad):
    return (low(grad),)
low.defvjp(low_keep, low_pass)
low_back.defvjp(back_keep, back_low)

def matmul(left, right):
    return jnp.dot(left, right, precision=lax.Precision.HIGHEST, preferred_element_type=jnp.float32)

def norm_rows(hidden, norm_gain):
    factor = lax.rsqrt(lax.optimization_barrier(jnp.mean(hidden * hidden, axis=-1, keepdims=True)) + epsilon)
    return hidden * factor * norm_gain

def conv_silu(inner, conv_kernel, conv_bias):
    taps = conv_kernel.shape[0]
    length = inner.shape[1]
    padded = jnp.pad(inner, ((0, 0), (taps - 1, 0), (0, 0)))
    total = jnp.broadcast_to(conv_bias, inner.shape)
    for offset in range(taps):
        total = total + conv_kernel[offset] * padded[:, offset:offset + length]
    return jax.nn.silu(total)

def span_step(decay_rate, state, block):
    delta, drive_in, read_out, inner = block
    outputs = []
    for position in range(delta.shape[1]):
        step_delta = delta[:, position]
        decay = jnp.exp(step_delta[:, None, :] * decay_rate)
        drive = (step_delta * inner[:, position])[:, None, :] * drive_in[:, position, :, None]
        state = decay * state + drive
        outputs.append(lax.optimization_barrier(jnp.sum(read_out[:, position, :, None] * state, axis=1)))
    return (state, jnp.stack(outputs, axis=1))

def selective(delta, drive_in, read_out, inner, decay_rate):
    batch, length, channels = delta.shape
    count = length // SPAN

    def blocks(value):
        return jnp.swapaxes(value.reshape(batch, count, SPAN, value.shape[-1]), 0, 1)
    stepper = jax.checkpoint(partial(span_step, decay_rate))
    start = jnp.zeros((batch, decay_rate.shape[0], channels), jnp.float32)
    final, results = lax.scan(stepper, start, (blocks(delta), blocks(drive_in), blocks(read_out), blocks(inner)))
    return jnp.swapaxes(results, 0, 1).reshape(batch, length, channels)

def mixer_core(step_pre, step_bias, decay_log, tail, inner, gate_in, skip_gain):
    delta = jax.nn.softplus(step_pre + step_bias)
    decay_rate = -jnp.exp(decay_log)
    states = decay_log.shape[0]
    output = selective(delta, tail[..., :states], tail[..., states:], inner, decay_rate)
    output = output + skip_gain * inner
    return output * jax.nn.silu(gate_in)

def layer(hidden, mask, params):
    norm_gain, in_proj, conv_kernel, conv_bias, x_proj, step_proj, step_bias, decay_log, skip_gain, out_proj = params
    normed = low(norm_rows(hidden, norm_gain))
    joined = low_back(matmul(normed, in_proj.reshape(D, 2 * E)))
    inner = low(conv_silu(joined[None, :, :E], conv_kernel, conv_bias)[0])
    mixed_in = low_back(matmul(inner, x_proj.T))
    step_low = low(mixed_in[:, :R])
    step_pre = low_back(matmul(step_low, step_proj))
    gated = mixer_core(step_pre[None], step_bias, decay_log, mixed_in[None, :, R:], inner[None], joined[None, :, E:], skip_gain)[0]
    branch = low_back(matmul(low(gated), out_proj))
    return hidden + mask * branch

def reference(tokens, lengths, cotangent, norm_gain, in_proj, conv_kernel, conv_bias, x_proj, step_proj, step_bias, decay_log, skip_gain, out_proj):
    params = tuple((weight.astype(jnp.float32) for weight in (norm_gain, in_proj, conv_kernel, conv_bias, x_proj, step_proj, step_bias, decay_log, skip_gain, out_proj)))
    rows = tokens.astype(jnp.float32).reshape(CLUSTERS, SLOTS, D)
    cot_rows = cotangent.astype(jnp.float32).reshape(CLUSTERS, SLOTS, D)
    place = jnp.arange(SLOTS, dtype=jnp.int32)

    def cluster(totals, item):
        hidden, cot_block, length = item
        mask = (place < length).astype(jnp.float32)[:, None]

        def forward(start, weights):
            current = start
            for index in range(LAYERS):
                current = layer(current, mask, tuple((weight[index] for weight in weights)))
            return current
        result, backward = jax.vjp(forward, hidden, params)
        grad_hidden, grad_params = backward(cot_block * mask)
        totals = tuple((total + grad for total, grad in zip(totals, grad_params)))
        return (totals, (result.astype(jnp.bfloat16), grad_hidden))
    zeros = tuple((jnp.zeros(weight.shape, jnp.float32) for weight in params))
    totals, (results, grads) = lax.scan(cluster, zeros, (rows, cot_rows, lengths))
    return (results.reshape(TOKENS, D), grads.reshape(TOKENS, D), totals[0], totals[1], totals[2], totals[3], totals[4], totals[5], totals[6], totals[7], totals[8], totals[9])
```

```python
import functools

import jax
import jax.numpy as jnp
from jax import lax
from jax.experimental import pallas as pl
from jax.experimental.pallas import tpu as pltpu
from jax.sharding import PartitionSpec as P

F32 = jnp.float32
BF16 = jnp.bfloat16
EPSILON = 1e-05
LOG2E = 1.4426950408889634
SLOTS = 128
STATES = 16
TAPS = 4
RANK = 64
SPAN = 16
WIDE = SPAN * STATES

NN = (((1,), (0,)), ((), ()))
NT = (((1,), (1,)), ((), ()))
TN = (((0,), (0,)), ((), ()))


def dot(left, right, dims=NN):
    return lax.dot_general(left, right, dims, preferred_element_type=F32)


def sigmoid(value):
    return 1.0 / (1.0 + jnp.exp(-value))


def softplus(value):
    return jnp.maximum(value, 0.0) + jnp.log1p(jnp.exp(-jnp.abs(value)))


def shift_rows(value, amount):
    slots = value.shape[0]
    if amount == 0:
        return value
    row = lax.broadcasted_iota(jnp.int32, value.shape, 0)
    moved = pltpu.roll(value, amount % slots, axis=0)
    keep = row >= amount if amount > 0 else row < slots + amount
    return jnp.where(keep, moved, 0.0)


def conv(inner, kernel, bias):
    total = bias + kernel[TAPS - 1 : TAPS] * inner
    for tap in range(TAPS - 1):
        total = total + kernel[tap : tap + 1] * shift_rows(inner, TAPS - 1 - tap)
    return total


def span_select(rows):
    row = lax.broadcasted_iota(jnp.int32, (rows, WIDE), 0)
    col = lax.broadcasted_iota(jnp.int32, (rows, WIDE), 1)
    return (row % SPAN) == (col // STATES)


def span_spread(values):
    rows = values.shape[0]
    state = lax.broadcasted_iota(jnp.int32, (STATES, WIDE), 0)
    col = lax.broadcasted_iota(jnp.int32, (STATES, WIDE), 1)
    tile = jnp.where(state == col % STATES, 1.0, 0.0).astype(BF16)
    spread = dot(values.astype(BF16), tile)
    return jnp.where(span_select(rows), spread, 0.0).astype(BF16)


def span_fold(rows, offset, width):
    row = lax.broadcasted_iota(jnp.int32, (WIDE, width), 0)
    col = lax.broadcasted_iota(jnp.int32, (WIDE, width), 1)
    return jnp.where(row % STATES == col - offset, 1.0, 0.0).astype(BF16)


def store_columns(scratch, values):
    rows, width = values.shape
    for tile in range(rows // SLOTS):
        part = values[tile * SLOTS : (tile + 1) * SLOTS, :]
        turned = jnp.transpose(part)
        for span in range(SLOTS // SPAN):
            moved = turned if span == 0 else pltpu.roll(turned, SLOTS - span * SPAN, axis=1)
            scratch[tile * (SLOTS // SPAN) + span] = moved[RANK : RANK + 2 * STATES, :]


def enter_kernel(h_ref, gain_ref, w_ref, ck_ref, cb_ref, xp_ref, x_ref, z_ref, u_ref, dbc_ref, hn_ref):
    step = pl.program_id(0)

    @pl.when(step == 0)
    def _():
        hidden = h_ref[...]
        factor = lax.rsqrt(jnp.mean(hidden * hidden, axis=-1, keepdims=True) + EPSILON)
        hn_ref[...] = (hidden * factor * gain_ref[...].astype(F32)).astype(BF16)
        dbc_ref[...] = jnp.zeros_like(dbc_ref)

    hn = hn_ref[...]
    x_ref[...] = dot(hn, w_ref[0, 0])
    z_ref[...] = dot(hn, w_ref[0, 1])
    kernel = ck_ref[0].astype(F32)
    bias = cb_ref[0].astype(F32)
    for cluster in range(h_ref.shape[0] // SLOTS):
        rows = pl.ds(cluster * SLOTS, SLOTS)
        c = conv(x_ref[rows, :], kernel, bias)
        u_ref[rows, :] = (c * sigmoid(c)).astype(BF16)
    dbc_ref[...] += dot(u_ref[...], xp_ref[0], NT)


def enter(layer, hidden, gain, w, ck, cb, xp, block):
    rows, width = hidden.shape
    channels = ck.shape[-1]
    grid = channels // block
    return pl.pallas_call(
        enter_kernel,
        grid=(grid,),
        in_specs=[
            pl.BlockSpec((rows, width), lambda j: (0, 0)),
            pl.BlockSpec((1, width), lambda j: (0, 0)),
            pl.BlockSpec((1, 2, width, block), lambda j: (layer, 0, 0, j)),
            pl.BlockSpec((1, TAPS, block), lambda j: (layer, 0, j)),
            pl.BlockSpec((1, 1, block), lambda j: (layer, 0, j)),
            pl.BlockSpec((1, RANK + 2 * STATES, block), lambda j: (layer, 0, j)),
        ],
        out_specs=[
            pl.BlockSpec((rows, block), lambda j: (0, j)),
            pl.BlockSpec((rows, block), lambda j: (0, j)),
            pl.BlockSpec((rows, block), lambda j: (0, j)),
            pl.BlockSpec((rows, RANK + 2 * STATES), lambda j: (0, 0)),
            pl.BlockSpec((rows, width), lambda j: (0, 0)),
        ],
        out_shape=[
            jax.ShapeDtypeStruct((rows, channels), F32),
            jax.ShapeDtypeStruct((rows, channels), F32),
            jax.ShapeDtypeStruct((rows, channels), BF16),
            jax.ShapeDtypeStruct((rows, RANK + 2 * STATES), F32),
            jax.ShapeDtypeStruct((rows, width), BF16),
        ],
        name="enter",
        cost_estimate=pl.CostEstimate(
            flops=4 * rows * width * channels, bytes_accessed=16 * rows * channels, transcendentals=rows * channels
        ),
    )(hidden, gain, w, ck, cb, xp)


def scan_kernel(
    dbc_ref, u_ref, z_ref, sp_ref, sb_ref, dl_ref, sk_ref, wo_ref,
    s_ref, y_ref, g_ref, o_ref,
    cols, cspan, delta, drive,
):
    step = pl.program_id(0)
    rows, block = u_ref.shape
    clusters = rows // SLOTS
    group = 2 if clusters % 2 == 0 else 1

    @pl.when(step == 0)
    def _():
        dbc = dbc_ref[...]
        padded = jnp.concatenate([dbc, jnp.zeros((rows, 128 - dbc.shape[1]), F32)], axis=1)
        store_columns(cols, padded)
        cspan[...] = span_spread(dbc[:, RANK + STATES :])
        o_ref[...] = jnp.zeros_like(o_ref)

    pre = dot(dbc_ref[:, :RANK].astype(BF16), sp_ref[0])
    u = u_ref[...].astype(F32)
    d = softplus(pre + sb_ref[0].astype(F32))
    delta[...] = d
    drive[...] = d * u
    rate = -jnp.exp(dl_ref[0].astype(F32)) * LOG2E

    for first in range(0, clusters, group):

        def body(span, states):
            states = list(states)
            columns = [
                cols[(first + k) * (SLOTS // SPAN) + span][:STATES, :] for k in range(group)
            ]
            for i in range(SPAN):
                for k in range(group):
                    t = (first + k) * SLOTS + span * SPAN + i
                    decay = jnp.exp2(delta[pl.ds(t, 1), :] * rate)
                    states[k] = decay * states[k] + drive[pl.ds(t, 1), :] * columns[k][:, i : i + 1]
                    at = pl.multiple_of(t * STATES, STATES)
                    s_ref[pl.ds(at, STATES), :] = states[k].astype(BF16)
            return tuple(states)

        lax.fori_loop(
            0, SLOTS // SPAN, body, tuple(jnp.zeros((STATES, block), F32) for _ in range(group))
        )

    for span in range(rows // SPAN):
        y_ref[span * SPAN : (span + 1) * SPAN, :] = dot(
            cspan[span * SPAN : (span + 1) * SPAN, :], s_ref[span * WIDE : (span + 1) * WIDE, :]
        )
    y = y_ref[...] + sk_ref[0].astype(F32) * u
    y_ref[...] = y
    z = z_ref[...]
    g = (y * (z * sigmoid(z))).astype(BF16)
    g_ref[...] = g
    o_ref[...] += dot(g, wo_ref[0])


def scan(layer, dbc, u, z, sp, sb, dl, sk, wo, block):
    rows, channels = u.shape
    width = wo.shape[-1]
    grid = channels // block
    tile = pl.BlockSpec((rows, block), lambda j: (0, j))
    return pl.pallas_call(
        scan_kernel,
        grid=(grid,),
        in_specs=[
            pl.BlockSpec(dbc.shape, lambda j: (0, 0)),
            tile,
            tile,
            pl.BlockSpec((1, RANK, block), lambda j: (layer, 0, j)),
            pl.BlockSpec((1, 1, block), lambda j: (layer, 0, j)),
            pl.BlockSpec((1, STATES, block), lambda j: (layer, 0, j)),
            pl.BlockSpec((1, 1, block), lambda j: (layer, 0, j)),
            pl.BlockSpec((1, block, width), lambda j: (layer, j, 0)),
        ],
        out_specs=[
            pl.BlockSpec((rows * STATES, block), lambda j: (0, j)),
            tile,
            tile,
            pl.BlockSpec((rows, width), lambda j: (0, 0)),
        ],
        out_shape=[
            jax.ShapeDtypeStruct((rows * STATES, channels), BF16),
            jax.ShapeDtypeStruct((rows, channels), F32),
            jax.ShapeDtypeStruct((rows, channels), BF16),
            jax.ShapeDtypeStruct((rows, width), F32),
        ],
        scratch_shapes=[
            pltpu.VMEM((rows // SPAN, 2 * STATES, 128), F32),
            pltpu.VMEM((rows, WIDE), BF16),
            pltpu.VMEM((rows, block), F32),
            pltpu.VMEM((rows, block), F32),
        ],
        name="scan",
        cost_estimate=pl.CostEstimate(
            flops=12 * rows * channels * STATES + 2 * rows * width * channels,
            bytes_accessed=48 * rows * channels,
            transcendentals=rows * channels * STATES,
        ),
    )(dbc, u, z, sp, sb, dl, sk, wo)


def back_scan_kernel(
    go_ref, dbc_ref, u_ref, z_ref, y_ref, s_ref, sp_ref, sb_ref, dl_ref, sk_ref, wo_ref,
    gz_ref, gu_ref, gdbc_ref, gsp_ref, gsb_ref, gdl_ref, gsk_ref,
    cols, bspan, delta, gy, lam, rot, accb, accc, gate,
):
    step = pl.program_id(0)
    last = pl.num_programs(0) - 1
    rows, block = u_ref.shape
    clusters = rows // SLOTS
    group = 2 if clusters % 2 == 0 else 1
    spans = SLOTS // SPAN

    @pl.when(step == 0)
    def _():
        dbc = dbc_ref[...]
        padded = jnp.concatenate([dbc, jnp.zeros((rows, 128 - dbc.shape[1]), F32)], axis=1)
        store_columns(cols, padded)
        bspan[...] = span_spread(dbc[:, RANK : RANK + STATES])
        gdbc_ref[...] = jnp.zeros_like(gdbc_ref)
        accb[...] = jnp.zeros_like(accb)
        accc[...] = jnp.zeros_like(accc)

    low = dbc_ref[:, :RANK].astype(BF16)
    raw = dot(low, sp_ref[0]) + sb_ref[0].astype(F32)
    delta[...] = softplus(raw)
    gate[...] = sigmoid(raw)

    gg = dot(go_ref[...], wo_ref[0], NT)
    z = z_ref[...]
    sig = sigmoid(z)
    gy[...] = gg * (z * sig)
    gz_ref[...] = (gg * y_ref[...] * (sig * (1.0 + z * (1.0 - sig)))).astype(BF16)

    base = -jnp.exp(dl_ref[0].astype(F32))
    rate = base * LOG2E
    total = jnp.zeros((STATES, block), F32)

    for first in range(0, clusters, group):

        def body(turn, carry):
            span = spans - 1 - turn
            total, carries = carry
            carries = list(carries)
            columns = [
                cols[(first + k) * spans + span][STATES:, :] for k in range(group)
            ]
            for i in reversed(range(SPAN)):
                for k in range(group):
                    t = (first + k) * SLOTS + span * SPAN + i
                    at = pl.multiple_of(t * STATES, STATES)
                    adjoint = columns[k][:, i : i + 1] * gy[pl.ds(t, 1), :] + carries[k]
                    lam[pl.ds(at, STATES), :] = adjoint.astype(BF16)
                    dt = delta[pl.ds(t, 1), :]
                    carries[k] = adjoint * jnp.exp2(dt * rate)
                    if i > 0:
                        before = s_ref[pl.ds(pl.multiple_of(at - STATES, STATES), STATES), :].astype(F32)
                    else:
                        where = pl.multiple_of(jnp.maximum(t - 1, 0) * STATES, STATES)
                        before = s_ref[pl.ds(where, STATES), :].astype(F32)
                        before = jnp.where(span > 0, before, 0.0)
                    turned = carries[k] * before
                    rot[pl.ds(at, STATES), :] = (base * turned).astype(BF16)
                    total = total + dt * turned
            return total, tuple(carries)

        total, _ = lax.fori_loop(
            0, spans, body, (total, tuple(jnp.zeros((STATES, block), F32) for _ in range(group)))
        )
    gdl_ref[...] = base * total

    u = u_ref[...].astype(F32)
    skip = sk_ref[0].astype(F32)
    drive = (delta[...] * u).astype(BF16)
    gyl = gy[...].astype(BF16)
    ones = jnp.where(span_select(SPAN), 1.0, 0.0).astype(BF16)
    gsk_ref[...] = jnp.sum(gy[...] * u, axis=0, keepdims=True)
    for span in range(rows // SPAN):
        small = slice(span * SPAN, (span + 1) * SPAN)
        wide = slice(span * WIDE, (span + 1) * WIDE)
        lams = lam[wide, :]
        gdrive = dot(bspan[small, :], lams)
        gturn = dot(ones, rot[wide, :])
        us = u[small]
        gu_ref[small, :] = delta[small, :] * gdrive + skip * gy[small, :]
        gate[small, :] = gate[small, :] * (us * gdrive + gturn)
        accb[small, :] += dot(drive[small], lams, NT)
        accc[small, :] += dot(gyl[small], s_ref[wide, :], NT)
    gpre = gate[...]
    gsb_ref[...] = jnp.sum(gpre, axis=0, keepdims=True)
    gpre = gpre.astype(BF16)
    gsp_ref[...] = dot(low, gpre, TN)
    gdbc_ref[:, :RANK] += dot(gpre, sp_ref[0], NT)

    @pl.when(step == last)
    def _():
        keep = span_select(rows)
        partb = jnp.where(keep, accb[...], 0.0).astype(BF16)
        partc = jnp.where(keep, accc[...], 0.0).astype(BF16)
        gdbc_ref[:, RANK:] = dot(partb, span_fold(WIDE, 0, 2 * STATES)) + dot(
            partc, span_fold(WIDE, STATES, 2 * STATES)
        )


def back_scan(layer, go, dbc, u, z, y, s, sp, sb, dl, sk, wo, block):
    rows, channels = u.shape
    width = wo.shape[-1]
    grid = channels // block
    tile = pl.BlockSpec((rows, block), lambda j: (0, j))
    return pl.pallas_call(
        back_scan_kernel,
        grid=(grid,),
        in_specs=[
            pl.BlockSpec(go.shape, lambda j: (0, 0)),
            pl.BlockSpec(dbc.shape, lambda j: (0, 0)),
            tile,
            tile,
            tile,
            pl.BlockSpec((rows * STATES, block), lambda j: (0, j)),
            pl.BlockSpec((1, RANK, block), lambda j: (layer, 0, j)),
            pl.BlockSpec((1, 1, block), lambda j: (layer, 0, j)),
            pl.BlockSpec((1, STATES, block), lambda j: (layer, 0, j)),
            pl.BlockSpec((1, 1, block), lambda j: (layer, 0, j)),
            pl.BlockSpec((1, block, width), lambda j: (layer, j, 0)),
        ],
        out_specs=[
            tile,
            tile,
            pl.BlockSpec(dbc.shape, lambda j: (0, 0)),
            pl.BlockSpec((RANK, block), lambda j: (0, j)),
            pl.BlockSpec((1, block), lambda j: (0, j)),
            pl.BlockSpec((STATES, block), lambda j: (0, j)),
            pl.BlockSpec((1, block), lambda j: (0, j)),
        ],
        out_shape=[
            jax.ShapeDtypeStruct((rows, channels), BF16),
            jax.ShapeDtypeStruct((rows, channels), F32),
            jax.ShapeDtypeStruct(dbc.shape, F32),
            jax.ShapeDtypeStruct((RANK, channels), F32),
            jax.ShapeDtypeStruct((1, channels), F32),
            jax.ShapeDtypeStruct((STATES, channels), F32),
            jax.ShapeDtypeStruct((1, channels), F32),
        ],
        scratch_shapes=[
            pltpu.VMEM((rows // SPAN, 2 * STATES, 128), F32),
            pltpu.VMEM((rows, WIDE), BF16),
            pltpu.VMEM((rows, block), F32),
            pltpu.VMEM((rows, block), F32),
            pltpu.VMEM((rows * STATES, block), BF16),
            pltpu.VMEM((rows * STATES, block), BF16),
            pltpu.VMEM((rows, WIDE), F32),
            pltpu.VMEM((rows, WIDE), F32),
            pltpu.VMEM((rows, block), F32),
        ],
        name="back_scan",
        cost_estimate=pl.CostEstimate(
            flops=24 * rows * channels * STATES + 2 * rows * width * channels,
            bytes_accessed=48 * rows * channels,
            transcendentals=rows * channels * STATES,
        ),
    )(go, dbc, u, z, y, s, sp, sb, dl, sk, wo)


def back_enter_kernel(
    gdbc_ref, gu_ref, x_ref, u_ref, gz_ref, ck_ref, cb_ref, xp_ref, w_ref,
    gx_ref, ghn_ref, gxp_ref, gck_ref, gcb_ref,
):
    step = pl.program_id(0)
    rows, block = u_ref.shape

    @pl.when(step == 0)
    def _():
        ghn_ref[...] = jnp.zeros_like(ghn_ref)

    gdbc = gdbc_ref[...].astype(BF16)
    gxp_ref[...] = dot(gdbc, u_ref[...], TN)
    kernel = ck_ref[0].astype(F32)
    bias = cb_ref[0].astype(F32)
    sums = [jnp.zeros((1, block), F32) for _ in range(TAPS)]
    sumb = jnp.zeros((1, block), F32)
    for cluster in range(rows // SLOTS):
        at = slice(cluster * SLOTS, (cluster + 1) * SLOTS)
        gu = gu_ref[at, :] + dot(gdbc[at], xp_ref[0])
        x = x_ref[at, :]
        moved = [shift_rows(x, TAPS - 1 - tap) for tap in range(TAPS)]
        c = bias
        for tap in range(TAPS):
            c = c + kernel[tap : tap + 1] * moved[tap]
        sig = sigmoid(c)
        gc = gu * (sig * (1.0 + c * (1.0 - sig)))
        gx = kernel[TAPS - 1 : TAPS] * gc
        for tap in range(TAPS):
            sums[tap] = sums[tap] + jnp.sum(gc * moved[tap], axis=0, keepdims=True)
            if tap < TAPS - 1:
                gx = gx + kernel[tap : tap + 1] * shift_rows(gc, tap - TAPS + 1)
        sumb = sumb + jnp.sum(gc, axis=0, keepdims=True)
        gx_ref[at, :] = gx.astype(BF16)
    gck_ref[...] = jnp.concatenate(sums, axis=0)
    gcb_ref[...] = sumb
    ghn_ref[...] += dot(gx_ref[...], w_ref[0, 0], NT) + dot(gz_ref[...], w_ref[0, 1], NT)


def back_enter(layer, gdbc, gu, x, u, gz, ck, cb, xp, w, block):
    rows, channels = u.shape
    width = w.shape[2]
    grid = channels // block
    tile = pl.BlockSpec((rows, block), lambda j: (0, j))
    low = RANK + 2 * STATES
    return pl.pallas_call(
        back_enter_kernel,
        grid=(grid,),
        in_specs=[
            pl.BlockSpec(gdbc.shape, lambda j: (0, 0)),
            tile,
            tile,
            tile,
            tile,
            pl.BlockSpec((1, TAPS, block), lambda j: (layer, 0, j)),
            pl.BlockSpec((1, 1, block), lambda j: (layer, 0, j)),
            pl.BlockSpec((1, low, block), lambda j: (layer, 0, j)),
            pl.BlockSpec((1, 2, width, block), lambda j: (layer, 0, 0, j)),
        ],
        out_specs=[
            tile,
            pl.BlockSpec((rows, width), lambda j: (0, 0)),
            pl.BlockSpec((low, block), lambda j: (0, j)),
            pl.BlockSpec((TAPS, block), lambda j: (0, j)),
            pl.BlockSpec((1, block), lambda j: (0, j)),
        ],
        out_shape=[
            jax.ShapeDtypeStruct((rows, channels), BF16),
            jax.ShapeDtypeStruct((rows, width), F32),
            jax.ShapeDtypeStruct((low, channels), F32),
            jax.ShapeDtypeStruct((TAPS, channels), F32),
            jax.ShapeDtypeStruct((1, channels), F32),
        ],
        name="back_enter",
        cost_estimate=pl.CostEstimate(
            flops=4 * rows * width * channels, bytes_accessed=24 * rows * channels, transcendentals=rows * channels
        ),
    )(gdbc, gu, x, u, gz, ck, cb, xp, w)


def body(groups, tokens, lengths, cotangent, norm_gain, in_proj, conv_kernel, conv_bias, x_proj,
         step_proj, step_bias, decay_log, skip_gain, out_proj):
    slots, width = tokens.shape
    layers = norm_gain.shape[0]
    channels = out_proj.shape[1]
    rows = groups * slots
    block = min(256, channels)
    me = lax.axis_index("fsdp")
    swap = [(i, groups - 1 - i) for i in range(groups)]

    def share(value):
        if groups == 2:
            return jnp.concatenate([value, lax.ppermute(value, "fsdp", swap)], axis=0)
        return lax.all_gather(value, "fsdp", axis=0, tiled=True)

    def all_sum(value, kind):
        if groups == 2:
            other = lax.ppermute(value.astype(kind), "fsdp", swap)
            return value + jnp.concatenate([other[slots:], other[:slots]], axis=0).astype(F32)
        return lax.psum(value.astype(kind), "fsdp").astype(F32)

    def mine(value):
        if groups == 2:
            return value[:slots]
        return lax.dynamic_slice_in_dim(value, me * slots, slots, 0)

    place = lax.broadcasted_iota(jnp.int32, (slots, 1), 0)
    mask = share(jnp.broadcast_to((place < lengths[0]).astype(F32), (slots, 128)))[:, :1]
    hidden = share(tokens).astype(F32)
    cot = share(cotangent)
    gains = lax.all_gather(norm_gain, "fsdp", axis=1, tiled=True)
    w = jnp.transpose(in_proj, (0, 2, 1, 3))
    cb = conv_bias[:, None]
    sb = step_bias[:, None]
    sk = skip_gain[:, None]

    saved = []
    for index in range(layers):
        gain = gains[index][None]
        x, z, u, dbc, hn = enter(index, hidden, gain, w, conv_kernel, cb, x_proj, block)
        dbc = all_sum(dbc, F32)
        s, y, g, branch = scan(index, dbc, u, z, step_proj, sb, decay_log, sk, out_proj, block)
        saved.append((hidden, x, z, u, dbc, hn, s, y, g))
        hidden = hidden + mask * all_sum(branch, BF16)
    mixed = mine(hidden).astype(BF16)

    grad = cot.astype(F32) * mask
    grads = [None] * layers
    for index in reversed(range(layers)):
        h, x, z, u, dbc, hn, s, y, g = saved[index]
        gain = gains[index].astype(F32)
        go = (grad * mask).astype(BF16)
        gz, gu, gdbc, gsp, gsb, gdl, gsk = back_scan(
            index, go, dbc, u, z, y, s, step_proj, sb, decay_log, sk, out_proj, block
        )
        gout = dot(g, go, TN)
        gdbc = all_sum(gdbc, F32)
        gx, ghn, gxp, gck, gcb = back_enter(
            index, gdbc, gu, x, u, gz, conv_kernel, cb, x_proj, w, block
        )
        ghn = all_sum(ghn, BF16)
        ginx = dot(hn, gx, TN)
        ginz = dot(hn, gz, TN)
        factor = lax.rsqrt(jnp.mean(h * h, axis=-1, keepdims=True) + EPSILON)
        scaled = ghn * gain
        ggain = jnp.sum(ghn * h * factor, axis=0)
        grad = grad + factor * scaled - h * (factor * factor * factor) * jnp.mean(
            scaled * h, axis=-1, keepdims=True
        )
        ggain = lax.dynamic_slice_in_dim(ggain, me * (width // groups), width // groups, 0)
        grads[index] = (
            ggain, jnp.stack([ginx, ginz], axis=1), gck, gcb[0], gxp, gsp, gsb[0], gdl, gsk[0], gout
        )
    tokens_grad = mine(grad)

    outs = []
    for member in range(10):
        outs.append(
            jnp.stack([lax.psum(grads[i][member].astype(BF16), "dp").astype(F32) for i in range(layers)])
        )
    return (mixed, tokens_grad) + tuple(outs)


def solution(mesh):
    rows = P(("dp", "fsdp"), None)
    in_specs = (
        rows,
        P(("dp", "fsdp")),
        rows,
        P(None, "fsdp"),
        P(None, None, None, "fsdp"),
        P(None, None, "fsdp"),
        P(None, "fsdp"),
        P(None, None, "fsdp"),
        P(None, None, "fsdp"),
        P(None, "fsdp"),
        P(None, None, "fsdp"),
        P(None, "fsdp"),
        P(None, "fsdp", None),
    )
    out_specs = (rows, rows) + in_specs[3:]
    return jax.shard_map(
        functools.partial(body, mesh.shape["fsdp"]),
        mesh=mesh, in_specs=in_specs, out_specs=out_specs, check_vma=False,
    )
```
